256 devices in a mesh: section: 4 (over x), tok: 64 (over y, z, core).
Axes of the slice: x: 4, y: 4, z: 8, core: 2. Of those that a mesh axis runs over, the one named last changes fastest.
Arguments:
- tracks: bfloat16 [4, 64, 128, 512], P('section', 'tok'), may hold values from -6 to 6
- valid_steps: int32 [4, 64, 128], P(None, 'tok'), may hold values from 0 to 1, as said below
- hilbert_order: int32 [4, 64], replicated, may hold values from 0 to 63, as said below
- temporal_gain: bfloat16 [4, 512], P('section'), may hold values from 0.099609375 to 1.8984375
- temporal_qkv: bfloat16 [4, 512, 1536], P('section'), may hold values from -7 to 7
- temporal_out: bfloat16 [4, 512, 512], P('section'), may hold values from -0.25 to 0.25
- social_gain: bfloat16 [4, 512], P('section'), may hold values from 0.099609375 to 1.8984375
- social_qkv: bfloat16 [4, 512, 1536], P('section'), may hold values from -7 to 7
- social_out: bfloat16 [4, 512, 512], P('section'), may hold values from -0.25 to 0.25
Outputs:
- evolved: bfloat16 [4, 64, 128, 512], P('section', 'tok')
The draws below stay inside these ranges and needn't reach their ends.
Inputs may be any that keep to these rules, and one draw needn't show every extreme that they name: `valid_steps`: each pedestrian's observed steps lie within one run of consecutive steps; any steps of that run, at its ends too and several in a row, may be unobserved. `hilbert_order`: each row names every pedestrian of the micro-batch once.
All inputs are finite; a program needn't handle non-finite values.
Results may differ from the reference program's by a relative error of at most 0.029.
Values may be sent and summed in bfloat16 or wider, within the bound.
A program may use at most 128 MiB of HBM per device.

```python
import jax
import jax.numpy as jnp
from jax import lax

D = 512
H = 8
HD = 64
T_SIZE = 128
TW = 32
SW = 128
A = 64
MB = 4
LAYERS = 4


def curve_permutations(key):
    batch_keys = jax.random.split(jax.random.fold_in(key, 11), MB)
    return jax.vmap(lambda single: jax.random.permutation(single, A))(batch_keys).astype(jnp.int32)


def draw_hilbert_order(key, part):
    return curve_permutations(key)


def draw_valid_steps(key, part):
    key_first = jax.random.fold_in(key, 21)
    key_length = jax.random.fold_in(key, 22)
    key_whole = jax.random.fold_in(key, 23)
    key_missing = jax.random.fold_in(key, 24)
    first_step = jax.random.randint(key_first, (MB, A, 1), 0, T_SIZE // 2)
    track_len = jax.random.randint(key_length, (MB, A, 1), T_SIZE // 4, T_SIZE + 1)
    whole_track = jax.random.randint(key_whole, (MB, A, 1), 0, 4) == 0
    first_step = jnp.where(whole_track, 0, first_step)
    last_step = jnp.where(whole_track, T_SIZE, jnp.minimum(first_step + track_len, T_SIZE))
    step_ids = jnp.arange(T_SIZE, dtype=jnp.int32)[None, None, :]
    missing = jax.random.randint(key_missing, (MB, A, T_SIZE), 0, 8) == 0
    observed = (step_ids >= first_step) & (step_ids < last_step) & jnp.logical_not(missing)
    return observed.astype(jnp.int32)


def draw_tracks(key, part):
    full_shape = (MB, A, T_SIZE, D)
    sample = jnp.clip(jax.random.normal(jax.random.fold_in(key, 1), full_shape, jnp.float32), -6.0, 6.0)
    return sample.astype(jnp.bfloat16)


def qkv_weights(key, salt):
    full_shape = (LAYERS, D, 3 * D)
    sample = jax.random.normal(jax.random.fold_in(key, salt), full_shape, jnp.float32) * D ** (-0.5)
    return sample.astype(jnp.bfloat16)


def draw_temporal_qkv(key, part):
    return qkv_weights(key, 31)


def draw_social_qkv(key, part):
    return qkv_weights(key, 32)


def block_levels(stream_key, extent, shards, low, high):
    def one(position, parts):
        heights = jax.random.uniform(jax.random.fold_in(jax.random.fold_in(stream_key, 6), position), (parts,), jnp.float32, low / len(shards), high / len(shards))
        return jnp.repeat(jnp.exp(heights), extent[position] // parts).reshape((-1,) + (1,) * (len(extent) - position - 1))

    factor_of = one(*shards[0])
    for cut in shards[1:]:
        factor_of = factor_of * one(*cut)
    return factor_of


def centred(rng, extent, scale, limit, cuts=(), held_as=jnp.bfloat16):
    factor_of = block_levels(rng, extent, cuts, -0.22, 0.18) if cuts else 1.0
    values = jax.random.normal(rng, extent, jnp.float32) * scale * factor_of
    return jnp.minimum(jnp.maximum(values, -limit), limit).astype(held_as)


def setup_inputs(seed: int = 0) -> dict:
    key_list = jax.random.split(jax.random.key(seed), 10)
    return {
        "tracks": draw_tracks(jax.random.fold_in(key_list[9], 71), 0),
        "valid_steps": draw_valid_steps(jax.random.fold_in(key_list[9], 71), 0),
        "hilbert_order": draw_hilbert_order(jax.random.fold_in(key_list[9], 71), 0),
        "temporal_gain": jnp.clip(1.0 + 0.18 * jax.random.normal(key_list[3], (LAYERS, D), jnp.float32), 0.099609375, 1.8984375).astype(jnp.bfloat16),
        "temporal_qkv": draw_temporal_qkv(jax.random.fold_in(key_list[9], 71), 0),
        "temporal_out": centred(key_list[5], (LAYERS, D, D), D ** -0.5, 0.25, ((0, 4),)),
        "social_gain": jnp.clip(1.0 + 0.18 * jax.random.normal(key_list[6], (LAYERS, D), jnp.float32), 0.099609375, 1.8984375).astype(jnp.bfloat16),
        "social_qkv": draw_social_qkv(jax.random.fold_in(key_list[9], 71), 0),
        "social_out": centred(key_list[8], (LAYERS, D, D), D ** -0.5, 0.25, ((0, 4),)),
    }


NEG_BIG = -1e+30
EPSILON = 1e-05

def rms_norm(rows, norm_gain):
    wide = rows.astype(jnp.float32)
    inverse_rms = lax.rsqrt(lax.optimization_barrier(jnp.mean(wide * wide, axis=-1, keepdims=True)) + EPSILON)
    return (wide * inverse_rms * norm_gain.astype(jnp.float32)).astype(jnp.bfloat16)

def soft_weights(scores, allowed):
    masked = jnp.where(allowed, scores, NEG_BIG)
    highest = lax.optimization_barrier(jnp.max(masked, axis=-1, keepdims=True))
    expon = jnp.exp(masked - highest)
    return (expon / lax.optimization_barrier(jnp.sum(expon, axis=-1, keepdims=True))).astype(jnp.bfloat16)

def temporal_sub(current, live_steps, norm_gain, weight_qkv, weight_out):
    later_idx = jnp.arange(T_SIZE, dtype=jnp.int32)[:, None]
    earlier = jnp.arange(T_SIZE, dtype=jnp.int32)[None, :]
    offset = later_idx - earlier

    def one_agent(inputs):
        agent_rows, agent_live = inputs
        normed = rms_norm(agent_rows, norm_gain)
        projected = jnp.dot(normed, weight_qkv, preferred_element_type=jnp.float32).astype(jnp.bfloat16)
        queries = projected[:, :D].reshape(T_SIZE, H, HD).astype(jnp.float32)
        key_rows = projected[:, D:2 * D].reshape(T_SIZE, H, HD).astype(jnp.float32)
        value_rows = projected[:, 2 * D:].reshape(T_SIZE, H, HD).astype(jnp.float32)
        scores = jnp.einsum('thd,shd->hts', queries, key_rows) * HD ** (-0.5)
        allowed = (offset >= 0) & (offset < TW) & ((agent_live[None, :] == 1) | (offset == 0))
        attn = soft_weights(scores, allowed[None])
        blended = jnp.einsum('hts,shd->thd', attn.astype(jnp.float32), value_rows).astype(jnp.bfloat16).reshape(T_SIZE, D)
        update = jnp.dot(blended, weight_out, preferred_element_type=jnp.float32)
        return (agent_rows.astype(jnp.float32) + update).astype(jnp.bfloat16)
    return lax.map(one_agent, (current, live_steps))

def social_sub(current, live_steps, curve_order, norm_gain, weight_qkv, weight_out):
    inverse = jnp.zeros((A,), jnp.int32).at[curve_order].set(jnp.arange(A, dtype=jnp.int32))
    positions = jnp.arange(A, dtype=jnp.int32)
    distance = positions[:, None] - positions[None, :]

    def one_step(inputs):
        step_rows, step_live = inputs
        ordered_rows = step_rows[curve_order]
        ordered_live = step_live[curve_order]
        normed = rms_norm(ordered_rows, norm_gain)
        projected = jnp.dot(normed, weight_qkv, preferred_element_type=jnp.float32).astype(jnp.bfloat16)
        queries = projected[:, :D].reshape(A, H, HD).astype(jnp.float32)
        key_rows = projected[:, D:2 * D].reshape(A, H, HD).astype(jnp.float32)
        value_rows = projected[:, 2 * D:].reshape(A, H, HD).astype(jnp.float32)
        scores = jnp.einsum('ihd,jhd->hij', queries, key_rows) * HD ** (-0.5)
        allowed = (jnp.abs(distance) <= SW) & ((ordered_live[None, :] == 1) | (distance == 0))
        attn = soft_weights(scores, allowed[None])
        blended = jnp.einsum('hij,jhd->ihd', attn.astype(jnp.float32), value_rows).astype(jnp.bfloat16).reshape(A, D)
        update = jnp.dot(blended, weight_out, preferred_element_type=jnp.float32)
        result_rows = (ordered_rows.astype(jnp.float32) + update).astype(jnp.bfloat16)
        return result_rows[inverse]
    moved = lax.map(one_step, (jnp.swapaxes(current, 0, 1), jnp.swapaxes(live_steps, 0, 1)))
    return jnp.swapaxes(moved, 0, 1)

def reference(tracks, valid_steps, hilbert_order, temporal_gain, temporal_qkv, temporal_out, social_gain, social_qkv, social_out):
    results = []
    for micro in range(tracks.shape[0]):
        current = tracks[micro]
        for layer_index in range(temporal_qkv.shape[0]):
            current = temporal_sub(current, valid_steps[micro], temporal_gain[layer_index], temporal_qkv[layer_index], temporal_out[layer_index])
            current = social_sub(current, valid_steps[micro], hilbert_order[micro], social_gain[layer_index], social_qkv[layer_index], social_out[layer_index])
        results.append(current)
    return jnp.stack(results)
```

```python
import functools

import jax
import jax.numpy as jnp
from jax import lax
from jax.experimental import pallas as pl
from jax.experimental.pallas import tpu as pltpu
from jax.sharding import PartitionSpec as P

H = 8
TW = 32
SW = 128
NEG_BIG = -1e30
EPSILON = 1e-05
MESH = pl.DeviceIdType.MESH
BF = jnp.bfloat16
F32 = jnp.float32


def sub_layer(src, gain, weight_qkv, weight_out, bias, stage):
    blocks, per_block, width = src.shape
    count = blocks * per_block
    head = width // H
    pair = 2 * head
    wide = src[...].reshape(count, width).astype(F32)
    inverse_rms = lax.rsqrt(jnp.mean(wide * wide, axis=-1, keepdims=True) + EPSILON)
    normed = (wide * inverse_rms * gain[...].astype(F32)).astype(BF)
    low = lax.broadcasted_iota(jnp.int32, (count, pair), 1) < head
    zero = jnp.zeros((count, pair), BF)
    bias_rows = bias[...]
    mixed = []
    group = 2 * pair
    for start in range(0, width, group):
        three = [
            jnp.dot(normed, weight_qkv[:, part * width + start : part * width + start + group],
                    preferred_element_type=F32)
            for part in range(3)
        ]
        query = (three[0] * head ** (-0.5)).astype(BF)
        key, value = three[1].astype(BF), three[2].astype(BF)
        for inner in range(0, group, pair):
            q = query[:, inner : inner + pair]
            k = key[:, inner : inner + pair]
            v = value[:, inner : inner + pair]
            both = jnp.concatenate([jnp.where(low, q, zero), jnp.where(low, zero, q)], axis=0)
            scores = lax.dot_general(both, k, (((1,), (1,)), ((), ())), preferred_element_type=F32)
            weights, sums = [], []
            for half in range(2):
                masked = scores[half * count : (half + 1) * count] + bias_rows
                expon = jnp.exp(masked - jnp.max(masked, axis=-1, keepdims=True))
                sums.append(jnp.sum(expon, axis=-1, keepdims=True))
                weights.append(expon.astype(BF))
            values = jnp.concatenate([jnp.where(low, v, zero), jnp.where(low, zero, v)], axis=0)
            blended = jnp.dot(jnp.concatenate(weights, axis=1), values, preferred_element_type=F32)
            scale = jnp.where(low, 1.0 / sums[0], 1.0 / sums[1])
            mixed.append((blended * scale).astype(BF))
    update = jnp.dot(jnp.concatenate(mixed, axis=1), weight_out[...], preferred_element_type=F32)
    stage[...] = (wide + update).astype(BF).reshape(blocks, per_block, width)


def kernel(
    sections, ways,
    tracks, valid, order, time_gain, crowd_gain,
    time_qkv_hbm, time_out_hbm, crowd_qkv_hbm, crowd_out_hbm,
    result,
    time_qkv, time_out, crowd_qkv, crowd_out,
    first, time_in, time_stage, crowd_in, crowd_stage, last_in,
    flag_stage, flag_in, time_bias, crowd_bias,
    weight_sem, first_sem, time_recv, time_send, crowd_recv, crowd_send,
    last_recv, flag_recv, flag_send, ready,
):
    section = lax.axis_index("section")
    me = lax.axis_index("tok")
    batches = time_in.shape[0]
    steps, width = tracks.shape
    per = steps // ways
    rows = steps

    loads = [
        pltpu.make_async_copy(hbm.at[0], held, weight_sem.at[i])
        for i, (hbm, held) in enumerate(
            ((time_qkv_hbm, time_qkv), (time_out_hbm, time_out),
             (crowd_qkv_hbm, crowd_qkv), (crowd_out_hbm, crowd_out))
        )
    ]
    for load in loads:
        load.start()

    barrier = pltpu.get_barrier_semaphore()

    @pl.when(section == 0)
    def _():
        for other in range(1, sections):
            pl.semaphore_signal(barrier, inc=1, device_id=(other, me), device_id_type=MESH)

        @pl.loop(1, ways)
        def _(step):
            pl.semaphore_signal(
                barrier, inc=1, device_id=(0, (me + step) % ways), device_id_type=MESH
            )

    @pl.when(section != 0)
    def _():
        pl.semaphore_signal(barrier, inc=1, device_id=(0, me), device_id_type=MESH)

    @pl.when(section == 0)
    def _():
        time_in[0] = tracks[...].reshape(ways, per, width)

    @pl.when(section != 0)
    def _():
        first[...] = tracks[...].reshape(ways, per, width)

    def first_copy(batch):
        return pltpu.make_async_remote_copy(
            src_ref=first, dst_ref=time_in.at[batch], send_sem=first_sem,
            recv_sem=time_recv.at[batch], device_id=(0, me), device_id_type=MESH,
        )

    @pl.when(section != 0)
    def _():
        pl.semaphore_wait(barrier, 1)
        first_copy(section).start()

    later = lax.broadcasted_iota(jnp.int32, (rows, rows), 0)
    earlier = lax.broadcasted_iota(jnp.int32, (rows, rows), 1)
    offset = later - earlier
    for batch in range(batches):
        flags = valid[batch]
        allowed = (offset >= 0) & (offset < TW) & ((flags == 1) | (offset == 0))
        time_bias[batch] = jnp.where(allowed, 0.0, NEG_BIG)
        flag_stage[batch : batch + 1, :] = flags.astype(F32).astype(BF)

    loads[0].wait()
    loads[1].wait()

    def exchange(src, dst, send_sem, recv_sem, target):
        @pl.when(target == section)
        def _():
            pltpu.make_async_copy(src.at[me], dst.at[me], recv_sem).start()

        @pl.when(target != section)
        def _():
            pltpu.make_async_remote_copy(
                src_ref=src.at[me], dst_ref=dst.at[me], send_sem=send_sem,
                recv_sem=recv_sem, device_id=(target, me), device_id_type=MESH,
            ).start()

        @pl.loop(1, ways)
        def _(step):
            peer = (me + step) % ways
            pltpu.make_async_remote_copy(
                src_ref=src.at[peer], dst_ref=dst.at[me], send_sem=send_sem,
                recv_sem=recv_sem, device_id=(target, peer), device_id_type=MESH,
            ).start()

    def exchange_flags():
        pltpu.make_async_copy(flag_stage, flag_in.at[me], flag_recv).start()

        @pl.loop(1, ways)
        def _(step):
            pltpu.make_async_remote_copy(
                src_ref=flag_stage, dst_ref=flag_in.at[me], send_sem=flag_send,
                recv_sem=flag_recv, device_id=(section, (me + step) % ways),
                device_id_type=MESH,
            ).start()

    def arrived(dst, recv_sem):
        pltpu.make_async_copy(dst, dst, recv_sem).wait()

    def sent(src, send_sem, local):
        @pl.when(local)
        def _():
            part = src.at[pl.ds(0, ways - 1)]
            pltpu.make_async_copy(part, part, send_sem).wait()

        @pl.when(jnp.logical_not(local))
        def _():
            pltpu.make_async_copy(src, src, send_sem).wait()

    @pl.loop(0, batches)
    def _(batch):
        @pl.when((section != 0) | (batch != 0))
        def _():
            arrived(time_in.at[batch], time_recv.at[batch])

        sub_layer(time_in.at[batch], time_gain, time_qkv, time_out,
                  time_bias.at[batch], time_stage.at[batch])

        @pl.when((section == 0) & (batch == 0))
        def _():
            pl.semaphore_wait(barrier, ways - 1 + sections - 1)

        @pl.when((section != 0) & (batch == 0))
        def _():
            pl.semaphore_wait(ready, 1)

        exchange(time_stage.at[batch], crowd_in.at[batch], time_send.at[batch],
                 crowd_recv.at[batch], section)

        @pl.when(batch == 0)
        def _():
            @pl.when(section == 0)
            def _():
                @pl.loop(1, ways)
                def _(step):
                    pl.semaphore_signal(
                        ready, inc=1, device_id=(0, (me + step) % ways), device_id_type=MESH
                    )

            exchange_flags()

    loads[2].wait()
    loads[3].wait()

    @pl.when(section == 0)
    def _():
        pl.semaphore_wait(ready, ways - 1)
        for other in range(1, sections):
            pl.semaphore_signal(ready, inc=1, device_id=(other, me), device_id_type=MESH)

    arrived(flag_in, flag_recv)
    row_of = lax.broadcasted_iota(jnp.int32, (rows, rows), 0)
    col_of = lax.broadcasted_iota(jnp.int32, (rows, rows), 1)
    pick = (row_of == me * per + col_of % per).astype(F32).astype(BF)
    every = jnp.dot(flag_in[...].reshape(ways * batches, steps), pick, preferred_element_type=F32)
    pair_row = lax.broadcasted_iota(jnp.int32, (ways * batches, rows), 0)
    pair_col = lax.broadcasted_iota(jnp.int32, (ways * batches, rows), 1)
    agents = order.shape[1]
    who = lax.broadcasted_iota(jnp.int32, (rows, agents), 0) // per
    place = lax.broadcasted_iota(jnp.int32, (rows, agents), 1)
    same_step = row_of % per == col_of % per
    itself = row_of == col_of
    for batch in range(batches):
        own = pair_row == (pair_col // per) * batches + batch
        flags = jnp.sum(jnp.where(own, every, 0.0), axis=0, keepdims=True)
        curve_col = jnp.sum(
            jnp.where(order[batch : batch + 1, :] == who, place, 0), axis=1, keepdims=True
        )
        curve_row = jnp.sum(jnp.where(itself, curve_col, 0), axis=0, keepdims=True)
        in_band = jnp.abs(curve_col - curve_row) <= SW
        allowed = same_step & in_band & ((flags == 1.0) | itself)
        crowd_bias[batch] = jnp.where(allowed, 0.0, NEG_BIG)

    @pl.loop(0, batches)
    def _(batch):
        arrived(crowd_in.at[batch], crowd_recv.at[batch])
        sub_layer(crowd_in.at[batch], crowd_gain, crowd_qkv, crowd_out,
                  crowd_bias.at[batch], crowd_stage.at[batch])

        @pl.when(section < sections - 1)
        def _():
            exchange(crowd_stage.at[batch], time_in.at[batch], crowd_send.at[batch],
                     time_recv.at[batch], section + 1)

        @pl.when(section == sections - 1)
        def _():
            exchange(crowd_stage.at[batch], last_in, crowd_send.at[batch], last_recv, batch)

    arrived(last_in, last_recv)
    result[...] = last_in[...].reshape(steps, width)

    @pl.when(section != 0)
    def _():
        first_copy(section).wait_send()

    part = flag_in.at[pl.ds(0, ways - 1)]
    pltpu.make_async_copy(part, part, flag_send).wait()

    @pl.loop(0, batches)
    def _(batch):
        part = time_stage.at[batch, pl.ds(0, ways - 1)]
        pltpu.make_async_copy(part, part, time_send.at[batch]).wait()
        sent(crowd_stage.at[batch], crowd_send.at[batch],
             (section == sections - 1) & (batch == sections - 1))


def body(
    tracks, valid_steps, hilbert_order,
    temporal_gain, temporal_qkv, temporal_out,
    social_gain, social_qkv, social_out,
):
    sections, ways = lax.axis_size("section"), lax.axis_size("tok")
    _, _, steps, width = tracks.shape
    batches = valid_steps.shape[0]
    per = steps // ways
    block = (ways, per, width)
    vmem = pl.BlockSpec(memory_space=pltpu.VMEM)
    hbm = pl.BlockSpec(memory_space=pltpu.HBM)
    dma = pltpu.SemaphoreType.DMA
    out = pl.pallas_call(
        functools.partial(kernel, sections, ways),
        out_shape=jax.ShapeDtypeStruct((steps, width), BF),
        in_specs=[vmem] * 5 + [hbm] * 4,
        out_specs=vmem,
        scratch_shapes=[
            pltpu.VMEM(temporal_qkv.shape[1:], BF),
            pltpu.VMEM(temporal_out.shape[1:], BF),
            pltpu.VMEM(social_qkv.shape[1:], BF),
            pltpu.VMEM(social_out.shape[1:], BF),
            pltpu.VMEM(block, BF),
            pltpu.VMEM((batches,) + block, BF),
            pltpu.VMEM((batches,) + block, BF),
            pltpu.VMEM((batches,) + block, BF),
            pltpu.VMEM((batches,) + block, BF),
            pltpu.VMEM(block, BF),
            pltpu.VMEM((batches, steps), BF),
            pltpu.VMEM((ways, batches, steps), BF),
            pltpu.VMEM((batches, steps, steps), F32),
            pltpu.VMEM((batches, steps, steps), F32),
            dma((4,)), dma, dma((batches,)), dma((batches,)), dma((batches,)), dma((batches,)),
            dma, dma, dma, pltpu.SemaphoreType.REGULAR,
        ],
        compiler_params=pltpu.CompilerParams(
            collective_id=0, has_side_effects=True, vmem_limit_bytes=48 * 1024 * 1024
        ),
        name="layers",
    )(
        tracks.reshape(steps, width), valid_steps, hilbert_order, temporal_gain, social_gain,
        temporal_qkv, temporal_out, social_qkv, social_out,
    )
    return out.reshape(tracks.shape)


def solution(mesh):
    placed = (
        P("section", "tok", None, None),
        P(None, "tok", None),
        P(),
        P("section", None),
        P("section", None, None),
        P("section", None, None),
        P("section", None),
        P("section", None, None),
        P("section", None, None),
    )
    return jax.shard_map(
        body, mesh=mesh, in_specs=placed, out_specs=P("section", "tok", None, None), check_vma=False
    )
```

```python
import functools

import jax
import jax.numpy as jnp
from jax import lax
from jax.experimental import pallas as pl
from jax.experimental.pallas import tpu as pltpu
from jax.sharding import PartitionSpec as P

H = 8
TW = 32
SW = 128
NEG_BIG = -1e30
EPSILON = 1e-05
MESH = pl.DeviceIdType.MESH
BF = jnp.bfloat16
F32 = jnp.float32


def sub_layer(src, gain, weight_qkv, weight_out, bias, stage):
    blocks, per_block, width = src.shape
    count = blocks * per_block
    head = width // H
    pair = 2 * head
    wide = src[...].reshape(count, width).astype(F32)
    inverse_rms = lax.rsqrt(jnp.mean(wide * wide, axis=-1, keepdims=True) + EPSILON)
    normed = (wide * inverse_rms * gain[...].astype(F32)).astype(BF)
    low = lax.broadcasted_iota(jnp.int32, (count, pair), 1) < head
    zero = jnp.zeros((count, pair), BF)
    bias_rows = bias[...]
    mixed = []
    group = 2 * pair
    for start in range(0, width, group):
        three = [
            jnp.dot(normed, weight_qkv[:, part * width + start : part * width + start + group],
                    preferred_element_type=F32)
            for part in range(3)
        ]
        query = (three[0] * head ** (-0.5)).astype(BF)
        key, value = three[1].astype(BF), three[2].astype(BF)
        for inner in range(0, group, pair):
            q = query[:, inner : inner + pair]
            k = key[:, inner : inner + pair]
            v = value[:, inner : inner + pair]
            both = jnp.concatenate([jnp.where(low, q, zero), jnp.where(low, zero, q)], axis=0)
            scores = lax.dot_general(both, k, (((1,), (1,)), ((), ())), preferred_element_type=F32)
            weights, sums = [], []
            for half in range(2):
                masked = scores[half * count : (half + 1) * count] + bias_rows
                expon = jnp.exp(masked - jnp.max(masked, axis=-1, keepdims=True))
                sums.append(jnp.sum(expon, axis=-1, keepdims=True))
                weights.append(expon.astype(BF))
            values = jnp.concatenate([jnp.where(low, v, zero), jnp.where(low, zero, v)], axis=0)
            blended = jnp.dot(jnp.concatenate(weights, axis=1), values, preferred_element_type=F32)
            scale = jnp.where(low, 1.0 / sums[0], 1.0 / sums[1])
            mixed.append((blended * scale).astype(BF))
    update = jnp.dot(jnp.concatenate(mixed, axis=1), weight_out[...], preferred_element_type=F32)
    stage[...] = (wide + update).astype(BF).reshape(blocks, per_block, width)


def kernel(
    sections, ways,
    tracks_hbm, valid_hbm, order_hbm, time_gain_hbm, crowd_gain_hbm,
    time_qkv_hbm, time_out_hbm, crowd_qkv_hbm, crowd_out_hbm,
    result,
    tracks, valid, order, time_gain, crowd_gain,
    time_qkv, time_out, crowd_qkv, crowd_out,
    first, time_in, time_stage, crowd_in, crowd_stage, last_in,
    flag_stage, flag_in, time_bias, crowd_bias,
    load_sem, first_sem, time_recv, time_send, crowd_recv, crowd_send,
    last_recv, flag_recv, flag_send, ready,
):
    section = lax.axis_index("section")
    me = lax.axis_index("tok")
    batches = time_in.shape[0]
    steps, width = tracks.shape
    per = steps // ways
    rows = steps

    loads = [
        pltpu.make_async_copy(hbm, held, load_sem.at[i])
        for i, (hbm, held) in enumerate((
            (tracks_hbm, tracks), (time_gain_hbm, time_gain), (valid_hbm, valid),
            (time_qkv_hbm.at[0], time_qkv), (time_out_hbm.at[0], time_out),
            (order_hbm, order), (crowd_gain_hbm, crowd_gain),
            (crowd_qkv_hbm.at[0], crowd_qkv), (crowd_out_hbm.at[0], crowd_out),
        ))
    ]
    for load in loads:
        load.start()
    tracks_load, gain_load, valid_load, qkv_load, out_load = loads[:5]

    barrier = pltpu.get_barrier_semaphore()

    @pl.when(section == 0)
    def _():
        for other in range(1, sections):
            pl.semaphore_signal(barrier, inc=1, device_id=(other, me), device_id_type=MESH)

        @pl.loop(1, ways)
        def _(step):
            pl.semaphore_signal(
                barrier, inc=1, device_id=(0, (me + step) % ways), device_id_type=MESH
            )

    @pl.when(section != 0)
    def _():
        pl.semaphore_signal(barrier, inc=1, device_id=(0, me), device_id_type=MESH)

    tracks_load.wait()

    @pl.when(section == 0)
    def _():
        time_in[0] = tracks[...].reshape(ways, per, width)

    @pl.when(section != 0)
    def _():
        first[...] = tracks[...].reshape(ways, per, width)

    def first_copy(batch):
        return pltpu.make_async_remote_copy(
            src_ref=first, dst_ref=time_in.at[batch], send_sem=first_sem,
            recv_sem=time_recv.at[batch], device_id=(0, me), device_id_type=MESH,
        )

    @pl.when(section != 0)
    def _():
        pl.semaphore_wait(barrier, 1)
        first_copy(section).start()

    later = lax.broadcasted_iota(jnp.int32, (rows, rows), 0)
    earlier = lax.broadcasted_iota(jnp.int32, (rows, rows), 1)
    offset = later - earlier
    valid_load.wait()
    for batch in range(batches):
        flags = valid[batch]
        allowed = (offset >= 0) & (offset < TW) & ((flags == 1) | (offset == 0))
        time_bias[batch] = jnp.where(allowed, 0.0, NEG_BIG)
        flag_stage[batch : batch + 1, :] = flags.astype(F32).astype(BF)

    gain_load.wait()
    qkv_load.wait()
    out_load.wait()

    def exchange(src, dst, send_sem, recv_sem, target):
        @pl.when(target == section)
        def _():
            pltpu.make_async_copy(src.at[me], dst.at[me], recv_sem).start()

        @pl.when(target != section)
        def _():
            pltpu.make_async_remote_copy(
                src_ref=src.at[me], dst_ref=dst.at[me], send_sem=send_sem,
                recv_sem=recv_sem, device_id=(target, me), device_id_type=MESH,
            ).start()

        @pl.loop(1, ways)
        def _(step):
            peer = (me + step) % ways
            pltpu.make_async_remote_copy(
                src_ref=src.at[peer], dst_ref=dst.at[me], send_sem=send_sem,
                recv_sem=recv_sem, device_id=(target, peer), device_id_type=MESH,
            ).start()

    def exchange_flags():
        pltpu.make_async_copy(flag_stage, flag_in.at[me], flag_recv).start()

        @pl.loop(1, ways)
        def _(step):
            pltpu.make_async_remote_copy(
                src_ref=flag_stage, dst_ref=flag_in.at[me], send_sem=flag_send,
                recv_sem=flag_recv, device_id=(section, (me + step) % ways),
                device_id_type=MESH,
            ).start()

    def arrived(dst, recv_sem):
        pltpu.make_async_copy(dst, dst, recv_sem).wait()

    def sent(src, send_sem, local):
        @pl.when(local)
        def _():
            part = src.at[pl.ds(0, ways - 1)]
            pltpu.make_async_copy(part, part, send_sem).wait()

        @pl.when(jnp.logical_not(local))
        def _():
            pltpu.make_async_copy(src, src, send_sem).wait()

    @pl.loop(0, batches)
    def _(batch):
        @pl.when((section != 0) | (batch != 0))
        def _():
            arrived(time_in.at[batch], time_recv.at[batch])

        sub_layer(time_in.at[batch], time_gain, time_qkv, time_out,
                  time_bias.at[batch], time_stage.at[batch])

        @pl.when((section == 0) & (batch == 0))
        def _():
            pl.semaphore_wait(barrier, ways - 1 + sections - 1)

        @pl.when((section != 0) & (batch == 0))
        def _():
            pl.semaphore_wait(ready, 1)

        exchange(time_stage.at[batch], crowd_in.at[batch], time_send.at[batch],
                 crowd_recv.at[batch], section)

        @pl.when(batch == 0)
        def _():
            @pl.when(section == 0)
            def _():
                @pl.loop(1, ways)
                def _(step):
                    pl.semaphore_signal(
                        ready, inc=1, device_id=(0, (me + step) % ways), device_id_type=MESH
                    )

            exchange_flags()

    for load in loads[5:]:
        load.wait()

    @pl.when(section == 0)
    def _():
        pl.semaphore_wait(ready, ways - 1)
        for other in range(1, sections):
            pl.semaphore_signal(ready, inc=1, device_id=(other, me), device_id_type=MESH)

    arrived(flag_in, flag_recv)
    row_of = lax.broadcasted_iota(jnp.int32, (rows, rows), 0)
    col_of = lax.broadcasted_iota(jnp.int32, (rows, rows), 1)
    pick = (row_of == me * per + col_of % per).astype(F32).astype(BF)
    every = jnp.dot(flag_in[...].reshape(ways * batches, steps), pick, preferred_element_type=F32)
    pair_row = lax.broadcasted_iota(jnp.int32, (ways * batches, rows), 0)
    pair_col = lax.broadcasted_iota(jnp.int32, (ways * batches, rows), 1)
    agents = order.shape[1]
    who = lax.broadcasted_iota(jnp.int32, (rows, agents), 0) // per
    place = lax.broadcasted_iota(jnp.int32, (rows, agents), 1)
    same_step = row_of % per == col_of % per
    itself = row_of == col_of
    for batch in range(batches):
        own = pair_row == (pair_col // per) * batches + batch
        flags = jnp.sum(jnp.where(own, every, 0.0), axis=0, keepdims=True)
        curve_col = jnp.sum(
            jnp.where(order[batch : batch + 1, :] == who, place, 0), axis=1, keepdims=True
        )
        curve_row = jnp.sum(jnp.where(itself, curve_col, 0), axis=0, keepdims=True)
        in_band = jnp.abs(curve_col - curve_row) <= SW
        allowed = same_step & in_band & ((flags == 1.0) | itself)
        crowd_bias[batch] = jnp.where(allowed, 0.0, NEG_BIG)

    @pl.loop(0, batches)
    def _(batch):
        arrived(crowd_in.at[batch], crowd_recv.at[batch])
        sub_layer(crowd_in.at[batch], crowd_gain, crowd_qkv, crowd_out,
                  crowd_bias.at[batch], crowd_stage.at[batch])

        @pl.when(section < sections - 1)
        def _():
            exchange(crowd_stage.at[batch], time_in.at[batch], crowd_send.at[batch],
                     time_recv.at[batch], section + 1)

        @pl.when(section == sections - 1)
        def _():
            exchange(crowd_stage.at[batch], last_in, crowd_send.at[batch], last_recv, batch)

    arrived(last_in, last_recv)
    result[...] = last_in[...].reshape(steps, width)

    @pl.when(section != 0)
    def _():
        first_copy(section).wait_send()

    part = flag_in.at[pl.ds(0, ways - 1)]
    pltpu.make_async_copy(part, part, flag_send).wait()

    @pl.loop(0, batches)
    def _(batch):
        part = time_stage.at[batch, pl.ds(0, ways - 1)]
        pltpu.make_async_copy(part, part, time_send.at[batch]).wait()
        sent(crowd_stage.at[batch], crowd_send.at[batch],
             (section == sections - 1) & (batch == sections - 1))


def body(
    tracks, valid_steps, hilbert_order,
    temporal_gain, temporal_qkv, temporal_out,
    social_gain, social_qkv, social_out,
):
    sections, ways = lax.axis_size("section"), lax.axis_size("tok")
    _, _, steps, width = tracks.shape
    batches = valid_steps.shape[0]
    per = steps // ways
    block = (ways, per, width)
    vmem = pl.BlockSpec(memory_space=pltpu.VMEM)
    hbm = pl.BlockSpec(memory_space=pltpu.HBM)
    dma = pltpu.SemaphoreType.DMA
    out = pl.pallas_call(
        functools.partial(kernel, sections, ways),
        out_shape=jax.ShapeDtypeStruct((steps, width), BF),
        in_specs=[hbm] * 9,
        out_specs=vmem,
        scratch_shapes=[
            pltpu.VMEM((steps, width), BF),
            pltpu.VMEM(valid_steps.shape, valid_steps.dtype),
            pltpu.VMEM(hilbert_order.shape, hilbert_order.dtype),
            pltpu.VMEM(temporal_gain.shape, BF),
            pltpu.VMEM(social_gain.shape, BF),
            pltpu.VMEM(temporal_qkv.shape[1:], BF),
            pltpu.VMEM(temporal_out.shape[1:], BF),
            pltpu.VMEM(social_qkv.shape[1:], BF),
            pltpu.VMEM(social_out.shape[1:], BF),
            pltpu.VMEM(block, BF),
            pltpu.VMEM((batches,) + block, BF),
            pltpu.VMEM((batches,) + block, BF),
            pltpu.VMEM((batches,) + block, BF),
            pltpu.VMEM((batches,) + block, BF),
            pltpu.VMEM(block, BF),
            pltpu.VMEM((batches, steps), BF),
            pltpu.VMEM((ways, batches, steps), BF),
            pltpu.VMEM((batches, steps, steps), F32),
            pltpu.VMEM((batches, steps, steps), F32),
            dma((9,)), dma, dma((batches,)), dma((batches,)), dma((batches,)), dma((batches,)),
            dma, dma, dma, pltpu.SemaphoreType.REGULAR,
        ],
        compiler_params=pltpu.CompilerParams(
            collective_id=0, has_side_effects=True, vmem_limit_bytes=67_043_328
        ),
        name="layers",
    )(
        tracks.reshape(steps, width), valid_steps, hilbert_order, temporal_gain, social_gain,
        temporal_qkv, temporal_out, social_qkv, social_out,
    )
    return out.reshape(tracks.shape)


def solution(mesh):
    placed = (
        P("section", "tok", None, None),
        P(None, "tok", None),
        P(),
        P("section", None),
        P("section", None, None),
        P("section", None, None),
        P("section", None),
        P("section", None, None),
        P("section", None, None),
    )
    return jax.shard_map(
        body, mesh=mesh, in_specs=placed, out_specs=P("section", "tok", None, None), check_vma=False
    )
```

```python
import functools

import jax
import jax.numpy as jnp
from jax import lax
from jax.experimental import pallas as pl
from jax.experimental.pallas import tpu as pltpu
from jax.sharding import PartitionSpec as P

H = 8
TW = 32
SW = 128
NEG_BIG = -1e30
EPSILON = 1e-05
MESH = pl.DeviceIdType.MESH
BF = jnp.bfloat16
F32 = jnp.float32


def sub_layer(src, gain, weight_qkv, weight_out, bias, stage):
    blocks, per_block, width = src.shape
    count = blocks * per_block
    head = width // H
    pair = 2 * head
    wide = src[...].reshape(count, width).astype(F32)
    inverse_rms = lax.rsqrt(jnp.mean(wide * wide, axis=-1, keepdims=True) + EPSILON)
    normed = (wide * inverse_rms * gain[...].astype(F32)).astype(BF)
    low = lax.broadcasted_iota(jnp.int32, (count, pair), 1) < head
    zero = jnp.zeros((count, pair), BF)
    bias_rows = bias[...]
    mixed = []
    group = 2 * pair
    for start in range(0, width, group):
        three = [
            jnp.dot(normed, weight_qkv[:, part * width + start : part * width + start + group],
                    preferred_element_type=F32)
            for part in range(3)
        ]
        query = (three[0] * head ** (-0.5)).astype(BF)
        key, value = three[1].astype(BF), three[2].astype(BF)
        for inner in range(0, group, pair):
            q = query[:, inner : inner + pair]
            k = key[:, inner : inner + pair]
            v = value[:, inner : inner + pair]
            both = jnp.concatenate([jnp.where(low, q, zero), jnp.where(low, zero, q)], axis=0)
            scores = lax.dot_general(both, k, (((1,), (1,)), ((), ())), preferred_element_type=F32)
            weights, sums = [], []
            for half in range(2):
                masked = scores[half * count : (half + 1) * count] + bias_rows
                expon = jnp.exp(masked - jnp.max(masked, axis=-1, keepdims=True))
                sums.append(jnp.sum(expon, axis=-1, keepdims=True))
                weights.append(expon.astype(BF))
            values = jnp.concatenate([jnp.where(low, v, zero), jnp.where(low, zero, v)], axis=0)
            blended = jnp.dot(jnp.concatenate(weights, axis=1), values, preferred_element_type=F32)
            scale = jnp.where(low, 1.0 / sums[0], 1.0 / sums[1])
            mixed.append((blended * scale).astype(BF))
    update = jnp.dot(jnp.concatenate(mixed, axis=1), weight_out[...], preferred_element_type=F32)
    stage[...] = (wide + update).astype(BF).reshape(blocks, per_block, width)


def kernel(
    sections, ways,
    tracks_hbm, valid_hbm, order_hbm, time_gain_hbm, crowd_gain_hbm,
    time_qkv_hbm, time_out_hbm, crowd_qkv_hbm, crowd_out_hbm,
    result,
    tracks, valid, order, time_gain, crowd_gain,
    time_qkv, time_out, crowd_qkv, crowd_out,
    first, time_in, time_stage, crowd_in, crowd_stage, last_in,
    flag_stage, flag_in, time_bias, crowd_bias,
    load_sem, first_sem, time_recv, time_send, crowd_recv, crowd_send,
    last_recv, flag_recv, flag_send, ready,
):
    section = lax.axis_index("section")
    me = lax.axis_index("tok")
    batches = time_in.shape[0]
    steps, width = tracks.shape
    per = steps // ways
    rows = steps

    loads = [
        pltpu.make_async_copy(hbm, held, load_sem.at[i])
        for i, (hbm, held) in enumerate((
            (tracks_hbm, tracks), (time_gain_hbm, time_gain), (valid_hbm, valid),
            (time_qkv_hbm.at[0], time_qkv), (time_out_hbm.at[0], time_out),
            (order_hbm, order), (crowd_gain_hbm, crowd_gain),
            (crowd_qkv_hbm.at[0], crowd_qkv), (crowd_out_hbm.at[0], crowd_out),
        ))
    ]
    for load in loads:
        load.start()
    tracks_load, gain_load, valid_load, qkv_load, out_load = loads[:5]

    barrier = pltpu.get_barrier_semaphore()

    @pl.when(section == 0)
    def _():
        for other in range(1, sections):
            pl.semaphore_signal(barrier, inc=1, device_id=(other, me), device_id_type=MESH)

        @pl.loop(1, ways)
        def _(step):
            pl.semaphore_signal(
                barrier, inc=1, device_id=(0, (me + step) % ways), device_id_type=MESH
            )

    @pl.when(section != 0)
    def _():
        pl.semaphore_signal(barrier, inc=1, device_id=(0, me), device_id_type=MESH)

    tracks_load.wait()

    @pl.when(section == 0)
    def _():
        time_in[0] = tracks[...].reshape(ways, per, width)

    @pl.when(section != 0)
    def _():
        first[...] = tracks[...].reshape(ways, per, width)

    def first_copy(batch):
        return pltpu.make_async_remote_copy(
            src_ref=first, dst_ref=time_in.at[batch], send_sem=first_sem,
            recv_sem=time_recv.at[batch], device_id=(0, me), device_id_type=MESH,
        )

    @pl.when(section != 0)
    def _():
        pl.semaphore_wait(barrier, 1)
        first_copy(section).start()

    later = lax.broadcasted_iota(jnp.int32, (rows, rows), 0)
    earlier = lax.broadcasted_iota(jnp.int32, (rows, rows), 1)
    offset = later - earlier
    valid_load.wait()
    for batch in range(batches):
        flags = valid[batch]
        allowed = (offset >= 0) & (offset < TW) & ((flags == 1) | (offset == 0))
        time_bias[batch] = jnp.where(allowed, 0.0, NEG_BIG)
        flag_stage[batch : batch + 1, :] = flags.astype(F32).astype(BF)

    gain_load.wait()
    qkv_load.wait()
    out_load.wait()

    def exchange(src, dst, send_sem, recv_sem, target):
        @pl.when(target == section)
        def _():
            pltpu.make_async_copy(src.at[me], dst.at[me], recv_sem).start()

        @pl.when(target != section)
        def _():
            pltpu.make_async_remote_copy(
                src_ref=src.at[me], dst_ref=dst.at[me], send_sem=send_sem,
                recv_sem=recv_sem, device_id=(target, me), device_id_type=MESH,
            ).start()

        @pl.loop(1, ways)
        def _(step):
            peer = (me + step) % ways
            pltpu.make_async_remote_copy(
                src_ref=src.at[peer], dst_ref=dst.at[me], send_sem=send_sem,
                recv_sem=recv_sem, device_id=(target, peer), device_id_type=MESH,
            ).start()

    def exchange_flags():
        pltpu.make_async_copy(flag_stage, flag_in.at[me], flag_recv).start()

        @pl.loop(1, ways)
        def _(step):
            pltpu.make_async_remote_copy(
                src_ref=flag_stage, dst_ref=flag_in.at[me], send_sem=flag_send,
                recv_sem=flag_recv, device_id=(section, (me + step) % ways),
                device_id_type=MESH,
            ).start()

    def arrived(dst, recv_sem):
        pltpu.make_async_copy(dst, dst, recv_sem).wait()

    def sent(src, send_sem, local):
        @pl.when(local)
        def _():
            part = src.at[pl.ds(0, ways - 1)]
            pltpu.make_async_copy(part, part, send_sem).wait()

        @pl.when(jnp.logical_not(local))
        def _():
            pltpu.make_async_copy(src, src, send_sem).wait()

    def temporal(batch):
        @pl.when((section != 0) | (batch != 0))
        def _():
            arrived(time_in.at[batch], time_recv.at[batch])

        sub_layer(time_in.at[batch], time_gain, time_qkv, time_out,
                  time_bias.at[batch], time_stage.at[batch])

        @pl.when((section == 0) & (batch == 0))
        def _():
            pl.semaphore_wait(barrier, ways - 1 + sections - 1)
            exchange_flags()

        exchange(time_stage.at[batch], crowd_in.at[batch], time_send.at[batch],
                 crowd_recv.at[batch], section)

        @pl.when((section == 0) & (batch == 0))
        def _():
            @pl.loop(1, ways)
            def _(step):
                pl.semaphore_signal(
                    ready, inc=1, device_id=(0, (me + step) % ways), device_id_type=MESH
                )

    def crowd_masks():
        for load in loads[5:]:
            load.wait()

        arrived(flag_in, flag_recv)
        row_of = lax.broadcasted_iota(jnp.int32, (rows, rows), 0)
        col_of = lax.broadcasted_iota(jnp.int32, (rows, rows), 1)
        pick = (row_of == me * per + col_of % per).astype(F32).astype(BF)
        every = jnp.dot(flag_in[...].reshape(ways * batches, steps), pick, preferred_element_type=F32)
        pair_row = lax.broadcasted_iota(jnp.int32, (ways * batches, rows), 0)
        pair_col = lax.broadcasted_iota(jnp.int32, (ways * batches, rows), 1)
        agents = order.shape[1]
        who = lax.broadcasted_iota(jnp.int32, (rows, agents), 0) // per
        place = lax.broadcasted_iota(jnp.int32, (rows, agents), 1)
        same_step = row_of % per == col_of % per
        itself = row_of == col_of
        for batch in range(batches):
            own = pair_row == (pair_col // per) * batches + batch
            flags = jnp.sum(jnp.where(own, every, 0.0), axis=0, keepdims=True)
            curve_col = jnp.sum(
                jnp.where(order[batch : batch + 1, :] == who, place, 0), axis=1, keepdims=True
            )
            curve_row = jnp.sum(jnp.where(itself, curve_col, 0), axis=0, keepdims=True)
            in_band = jnp.abs(curve_col - curve_row) <= SW
            allowed = same_step & in_band & ((flags == 1.0) | itself)
            crowd_bias[batch] = jnp.where(allowed, 0.0, NEG_BIG)

    def social(batch):
        arrived(crowd_in.at[batch], crowd_recv.at[batch])
        sub_layer(crowd_in.at[batch], crowd_gain, crowd_qkv, crowd_out,
                  crowd_bias.at[batch], crowd_stage.at[batch])

        @pl.when(section < sections - 1)
        def _():
            exchange(crowd_stage.at[batch], time_in.at[batch], crowd_send.at[batch],
                     time_recv.at[batch], section + 1)

        @pl.when(section == sections - 1)
        def _():
            exchange(crowd_stage.at[batch], last_in, crowd_send.at[batch], last_recv, batch)

    @pl.when(section != 0)
    def _():
        pl.semaphore_wait(ready, 1)
        exchange_flags()

    @pl.loop(0, batches + 1)
    def _(turn):
        @pl.when(turn < batches)
        def _():
            temporal(turn)

        @pl.when((section == 0) & (turn == 1))
        def _():
            pl.semaphore_wait(ready, ways - 1)
            for other in range(1, sections):
                pl.semaphore_signal(ready, inc=1, device_id=(other, me), device_id_type=MESH)

        @pl.when(((section == 0) & (turn == 1)) | ((section != 0) & (turn == 0)))
        def _():
            crowd_masks()

        @pl.when(turn > 0)
        def _():
            social(turn - 1)

    arrived(last_in, last_recv)
    result[...] = last_in[...].reshape(steps, width)

    @pl.when(section != 0)
    def _():
        first_copy(section).wait_send()

    part = flag_in.at[pl.ds(0, ways - 1)]
    pltpu.make_async_copy(part, part, flag_send).wait()

    @pl.loop(0, batches)
    def _(batch):
        part = time_stage.at[batch, pl.ds(0, ways - 1)]
        pltpu.make_async_copy(part, part, time_send.at[batch]).wait()
        sent(crowd_stage.at[batch], crowd_send.at[batch],
             (section == sections - 1) & (batch == sections - 1))


def body(
    tracks, valid_steps, hilbert_order,
    temporal_gain, temporal_qkv, temporal_out,
    social_gain, social_qkv, social_out,
):
    sections, ways = lax.axis_size("section"), lax.axis_size("tok")
    _, _, steps, width = tracks.shape
    batches = valid_steps.shape[0]
    per = steps // ways
    block = (ways, per, width)
    vmem = pl.BlockSpec(memory_space=pltpu.VMEM)
    hbm = pl.BlockSpec(memory_space=pltpu.HBM)
    dma = pltpu.SemaphoreType.DMA
    out = pl.pallas_call(
        functools.partial(kernel, sections, ways),
        out_shape=jax.ShapeDtypeStruct((steps, width), BF),
        in_specs=[hbm] * 9,
        out_specs=vmem,
        scratch_shapes=[
            pltpu.VMEM((steps, width), BF),
            pltpu.VMEM(valid_steps.shape, valid_steps.dtype),
            pltpu.VMEM(hilbert_order.shape, hilbert_order.dtype),
            pltpu.VMEM(temporal_gain.shape, BF),
            pltpu.VMEM(social_gain.shape, BF),
            pltpu.VMEM(temporal_qkv.shape[1:], BF),
            pltpu.VMEM(temporal_out.shape[1:], BF),
            pltpu.VMEM(social_qkv.shape[1:], BF),
            pltpu.VMEM(social_out.shape[1:], BF),
            pltpu.VMEM(block, BF),
            pltpu.VMEM((batches,) + block, BF),
            pltpu.VMEM((batches,) + block, BF),
            pltpu.VMEM((batches,) + block, BF),
            pltpu.VMEM((batches,) + block, BF),
            pltpu.VMEM(block, BF),
            pltpu.VMEM((batches, steps), BF),
            pltpu.VMEM((ways, batches, steps), BF),
            pltpu.VMEM((batches, steps, steps), F32),
            pltpu.VMEM((batches, steps, steps), F32),
            dma((9,)), dma, dma((batches,)), dma((batches,)), dma((batches,)), dma((batches,)),
            dma, dma, dma, pltpu.SemaphoreType.REGULAR,
        ],
        compiler_params=pltpu.CompilerParams(
            collective_id=0, has_side_effects=True, vmem_limit_bytes=67_043_328
        ),
        name="layers",
    )(
        tracks.reshape(steps, width), valid_steps, hilbert_order, temporal_gain, social_gain,
        temporal_qkv, temporal_out, social_qkv, social_out,
    )
    return out.reshape(tracks.shape)


def solution(mesh):
    placed = (
        P("section", "tok", None, None),
        P(None, "tok", None),
        P(),
        P("section", None),
        P("section", None, None),
        P("section", None, None),
        P("section", None),
        P("section", None, None),
        P("section", None, None),
    )
    return jax.shard_map(
        body, mesh=mesh, in_specs=placed, out_specs=P("section", "tok", None, None), check_vma=False
    )
```

```python
import functools

import jax
import jax.numpy as jnp
from jax import lax
from jax.experimental import pallas as pl
from jax.experimental.pallas import tpu as pltpu
from jax.sharding import PartitionSpec as P

H = 8
TW = 32
SW = 128
NEG_BIG = -1e30
EPSILON = 1e-05
MESH = pl.DeviceIdType.MESH
BF = jnp.bfloat16
F32 = jnp.float32


def sub_layer(src, gain, weight_qkv, weight_out, bias, stage):
    blocks, per_block, width = src.shape
    count = blocks * per_block
    head = width // H
    pair = 2 * head
    wide = src[...].reshape(count, width).astype(F32)
    inverse_rms = lax.rsqrt(jnp.mean(wide * wide, axis=-1, keepdims=True) + EPSILON)
    normed = (wide * inverse_rms * gain[...].astype(F32)).astype(BF)
    low = lax.broadcasted_iota(jnp.int32, (count, pair), 1) < head
    zero = jnp.zeros((count, pair), BF)
    bias_rows = bias[...]
    mixed = []
    group = 2 * pair
    for start in range(0, width, group):
        three = [
            jnp.dot(normed, weight_qkv[:, part * width + start : part * width + start + group],
                    preferred_element_type=F32)
            for part in range(3)
        ]
        query = (three[0] * head ** (-0.5)).astype(BF)
        key, value = three[1].astype(BF), three[2].astype(BF)
        for inner in range(0, group, pair):
            q = query[:, inner : inner + pair]
            k = key[:, inner : inner + pair]
            v = value[:, inner : inner + pair]
            both = jnp.concatenate([jnp.where(low, q, zero), jnp.where(low, zero, q)], axis=0)
            scores = lax.dot_general(both, k, (((1,), (1,)), ((), ())), preferred_element_type=F32)
            weights, sums = [], []
            for half in range(2):
                masked = scores[half * count : (half + 1) * count] + bias_rows
                expon = jnp.exp(masked - jnp.max(masked, axis=-1, keepdims=True))
                sums.append(jnp.sum(expon, axis=-1, keepdims=True))
                weights.append(expon.astype(BF))
            values = jnp.concatenate([jnp.where(low, v, zero), jnp.where(low, zero, v)], axis=0)
            blended = jnp.dot(jnp.concatenate(weights, axis=1), values, preferred_element_type=F32)
            scale = jnp.where(low, 1.0 / sums[0], 1.0 / sums[1])
            mixed.append((blended * scale).astype(BF))
    update = jnp.dot(jnp.concatenate(mixed, axis=1), weight_out[...], preferred_element_type=F32)
    stage[...] = (wide + update).astype(BF).reshape(blocks, per_block, width)


def kernel(
    sections, ways,
    tracks_hbm, valid_hbm, order_hbm, time_gain_hbm, crowd_gain_hbm,
    time_qkv_hbm, time_out_hbm, crowd_qkv_hbm, crowd_out_hbm,
    result,
    tracks, valid, order, time_gain, crowd_gain,
    time_qkv, time_out, crowd_qkv, crowd_out,
    first, time_in, time_stage, crowd_in, crowd_stage, last_in,
    flag_stage, flag_in, time_bias, crowd_bias,
    load_sem, first_sem, time_recv, time_send, crowd_recv, crowd_send,
    last_recv, flag_recv, flag_send, ready,
):
    section = lax.axis_index("section")
    me = lax.axis_index("tok")
    batches = time_in.shape[0]
    steps, width = tracks.shape
    per = steps // ways
    rows = steps

    loads = [
        pltpu.make_async_copy(hbm, held, load_sem.at[i])
        for i, (hbm, held) in enumerate((
            (tracks_hbm, tracks), (time_gain_hbm, time_gain), (valid_hbm, valid),
            (time_qkv_hbm.at[0], time_qkv), (time_out_hbm.at[0], time_out),
            (order_hbm, order), (crowd_gain_hbm, crowd_gain),
            (crowd_qkv_hbm.at[0], crowd_qkv), (crowd_out_hbm.at[0], crowd_out),
        ))
    ]
    for load in loads:
        load.start()
    tracks_load, gain_load, valid_load, qkv_load, out_load = loads[:5]

    barrier = pltpu.get_barrier_semaphore()

    @pl.when(section == 0)
    def _():
        for other in range(1, sections):
            pl.semaphore_signal(barrier, inc=1, device_id=(other, me), device_id_type=MESH)

        @pl.loop(1, ways)
        def _(step):
            pl.semaphore_signal(
                barrier, inc=1, device_id=(0, (me + step) % ways), device_id_type=MESH
            )

    @pl.when(section != 0)
    def _():
        pl.semaphore_signal(barrier, inc=1, device_id=(0, me), device_id_type=MESH)

    tracks_load.wait()

    @pl.when(section == 0)
    def _():
        time_in[0] = tracks[...].reshape(ways, per, width)

    @pl.when(section != 0)
    def _():
        first[...] = tracks[...].reshape(ways, per, width)

    def first_copy(batch):
        return pltpu.make_async_remote_copy(
            src_ref=first, dst_ref=time_in.at[batch], send_sem=first_sem,
            recv_sem=time_recv.at[batch], device_id=(0, me), device_id_type=MESH,
        )

    @pl.when(section != 0)
    def _():
        pl.semaphore_wait(barrier, 1)
        first_copy(section).start()

    later = lax.broadcasted_iota(jnp.int32, (rows, rows), 0)
    earlier = lax.broadcasted_iota(jnp.int32, (rows, rows), 1)
    offset = later - earlier
    valid_load.wait()
    for batch in range(batches):
        flags = valid[batch]
        allowed = (offset >= 0) & (offset < TW) & ((flags == 1) | (offset == 0))
        time_bias[batch] = jnp.where(allowed, 0.0, NEG_BIG)
        flag_stage[batch : batch + 1, :] = flags.astype(F32).astype(BF)

    gain_load.wait()
    qkv_load.wait()
    out_load.wait()

    def exchange(src, dst, send_sem, recv_sem, target):
        @pl.when(target == section)
        def _():
            pltpu.make_async_copy(src.at[me], dst.at[me], recv_sem).start()

        @pl.when(target != section)
        def _():
            pltpu.make_async_remote_copy(
                src_ref=src.at[me], dst_ref=dst.at[me], send_sem=send_sem,
                recv_sem=recv_sem, device_id=(target, me), device_id_type=MESH,
            ).start()

        @pl.loop(1, ways, unroll=3)
        def _(step):
            peer = (me + step) % ways
            pltpu.make_async_remote_copy(
                src_ref=src.at[peer], dst_ref=dst.at[me], send_sem=send_sem,
                recv_sem=recv_sem, device_id=(target, peer), device_id_type=MESH,
            ).start()

    def exchange_flags():
        pltpu.make_async_copy(flag_stage, flag_in.at[me], flag_recv).start()

        @pl.loop(1, ways)
        def _(step):
            pltpu.make_async_remote_copy(
                src_ref=flag_stage, dst_ref=flag_in.at[me], send_sem=flag_send,
                recv_sem=flag_recv, device_id=(section, (me + step) % ways),
                device_id_type=MESH,
            ).start()

    def arrived(dst, recv_sem):
        pltpu.make_async_copy(dst, dst, recv_sem).wait()

    def sent(src, send_sem, local):
        @pl.when(local)
        def _():
            part = src.at[pl.ds(0, ways - 1)]
            pltpu.make_async_copy(part, part, send_sem).wait()

        @pl.when(jnp.logical_not(local))
        def _():
            pltpu.make_async_copy(src, src, send_sem).wait()

    def temporal(batch):
        @pl.when((section != 0) | (batch != 0))
        def _():
            arrived(time_in.at[batch], time_recv.at[batch])

        sub_layer(time_in.at[batch], time_gain, time_qkv, time_out,
                  time_bias.at[batch], time_stage.at[batch])

        @pl.when((section == 0) & (batch == 0))
        def _():
            pl.semaphore_wait(barrier, ways - 1 + sections - 1)
            exchange_flags()

        exchange(time_stage.at[batch], crowd_in.at[batch], time_send.at[batch],
                 crowd_recv.at[batch], section)

        @pl.when((section == 0) & (batch == 0))
        def _():
            @pl.loop(1, ways)
            def _(step):
                pl.semaphore_signal(
                    ready, inc=1, device_id=(0, (me + step) % ways), device_id_type=MESH
                )

    def crowd_masks():
        for load in loads[5:]:
            load.wait()

        arrived(flag_in, flag_recv)
        row_of = lax.broadcasted_iota(jnp.int32, (rows, rows), 0)
        col_of = lax.broadcasted_iota(jnp.int32, (rows, rows), 1)
        pick = (row_of == me * per + col_of % per).astype(F32).astype(BF)
        every = jnp.dot(flag_in[...].reshape(ways * batches, steps), pick, preferred_element_type=F32)
        pair_row = lax.broadcasted_iota(jnp.int32, (ways * batches, rows), 0)
        pair_col = lax.broadcasted_iota(jnp.int32, (ways * batches, rows), 1)
        agents = order.shape[1]
        who = lax.broadcasted_iota(jnp.int32, (rows, agents), 0) // per
        place = lax.broadcasted_iota(jnp.int32, (rows, agents), 1)
        same_step = row_of % per == col_of % per
        itself = row_of == col_of
        for batch in range(batches):
            own = pair_row == (pair_col // per) * batches + batch
            flags = jnp.sum(jnp.where(own, every, 0.0), axis=0, keepdims=True)
            curve_col = jnp.sum(
                jnp.where(order[batch : batch + 1, :] == who, place, 0), axis=1, keepdims=True
            )
            curve_row = jnp.sum(jnp.where(itself, curve_col, 0), axis=0, keepdims=True)
            in_band = jnp.abs(curve_col - curve_row) <= SW
            allowed = same_step & in_band & ((flags == 1.0) | itself)
            crowd_bias[batch] = jnp.where(allowed, 0.0, NEG_BIG)

    def social(batch):
        arrived(crowd_in.at[batch], crowd_recv.at[batch])
        sub_layer(crowd_in.at[batch], crowd_gain, crowd_qkv, crowd_out,
                  crowd_bias.at[batch], crowd_stage.at[batch])

        @pl.when(section < sections - 1)
        def _():
            exchange(crowd_stage.at[batch], time_in.at[batch], crowd_send.at[batch],
                     time_recv.at[batch], section + 1)

        @pl.when(section == sections - 1)
        def _():
            exchange(crowd_stage.at[batch], last_in, crowd_send.at[batch], last_recv, batch)

    @pl.when(section != 0)
    def _():
        pl.semaphore_wait(ready, 1)
        exchange_flags()

    @pl.loop(0, batches + 1)
    def _(turn):
        @pl.when(turn < batches)
        def _():
            temporal(turn)

        @pl.when((section == 0) & (turn == 1))
        def _():
            pl.semaphore_wait(ready, ways - 1)
            for other in range(1, sections):
                pl.semaphore_signal(ready, inc=1, device_id=(other, me), device_id_type=MESH)

        @pl.when(((section == 0) & (turn == 1)) | ((section != 0) & (turn == 0)))
        def _():
            crowd_masks()

        @pl.when(turn > 0)
        def _():
            social(turn - 1)

    arrived(last_in, last_recv)
    result[...] = last_in[...].reshape(steps, width)

    @pl.when(section != 0)
    def _():
        first_copy(section).wait_send()

    part = flag_in.at[pl.ds(0, ways - 1)]
    pltpu.make_async_copy(part, part, flag_send).wait()

    @pl.loop(0, batches)
    def _(batch):
        part = time_stage.at[batch, pl.ds(0, ways - 1)]
        pltpu.make_async_copy(part, part, time_send.at[batch]).wait()
        sent(crowd_stage.at[batch], crowd_send.at[batch],
             (section == sections - 1) & (batch == sections - 1))


def body(
    tracks, valid_steps, hilbert_order,
    temporal_gain, temporal_qkv, temporal_out,
    social_gain, social_qkv, social_out,
):
    sections, ways = lax.axis_size("section"), lax.axis_size("tok")
    _, _, steps, width = tracks.shape
    batches = valid_steps.shape[0]
    per = steps // ways
    block = (ways, per, width)
    vmem = pl.BlockSpec(memory_space=pltpu.VMEM)
    hbm = pl.BlockSpec(memory_space=pltpu.HBM)
    dma = pltpu.SemaphoreType.DMA
    out = pl.pallas_call(
        functools.partial(kernel, sections, ways),
        out_shape=jax.ShapeDtypeStruct((steps, width), BF),
        in_specs=[hbm] * 9,
        out_specs=vmem,
        scratch_shapes=[
            pltpu.VMEM((steps, width), BF),
            pltpu.VMEM(valid_steps.shape, valid_steps.dtype),
            pltpu.VMEM(hilbert_order.shape, hilbert_order.dtype),
            pltpu.VMEM(temporal_gain.shape, BF),
            pltpu.VMEM(social_gain.shape, BF),
            pltpu.VMEM(temporal_qkv.shape[1:], BF),
            pltpu.VMEM(temporal_out.shape[1:], BF),
            pltpu.VMEM(social_qkv.shape[1:], BF),
            pltpu.VMEM(social_out.shape[1:], BF),
            pltpu.VMEM(block, BF),
            pltpu.VMEM((batches,) + block, BF),
            pltpu.VMEM((batches,) + block, BF),
            pltpu.VMEM((batches,) + block, BF),
            pltpu.VMEM((batches,) + block, BF),
            pltpu.VMEM(block, BF),
            pltpu.VMEM((batches, steps), BF),
            pltpu.VMEM((ways, batches, steps), BF),
            pltpu.VMEM((batches, steps, steps), F32),
            pltpu.VMEM((batches, steps, steps), F32),
            dma((9,)), dma, dma((batches,)), dma((batches,)), dma((batches,)), dma((batches,)),
            dma, dma, dma, pltpu.SemaphoreType.REGULAR,
        ],
        compiler_params=pltpu.CompilerParams(
            collective_id=0, has_side_effects=True, vmem_limit_bytes=67_043_328
        ),
        name="layers",
    )(
        tracks.reshape(steps, width), valid_steps, hilbert_order, temporal_gain, social_gain,
        temporal_qkv, temporal_out, social_qkv, social_out,
    )
    return out.reshape(tracks.shape)


def solution(mesh):
    placed = (
        P("section", "tok", None, None),
        P(None, "tok", None),
        P(),
        P("section", None),
        P("section", None, None),
        P("section", None, None),
        P("section", None),
        P("section", None, None),
        P("section", None, None),
    )
    return jax.shard_map(
        body, mesh=mesh, in_specs=placed, out_specs=P("section", "tok", None, None), check_vma=False
    )
```
